256 devices in a mesh: dp: 4 (over y), expert: 64 (over x, z, core).
Axes of the slice: x: 4, y: 4, z: 8, core: 2. Of those that a mesh axis runs over, the one named last changes fastest.
Arguments:
- tokens: bfloat16 [32768, 2048], P(('dp', 'expert')), may hold values from -6 to 6
- cotangent: bfloat16 [32768, 2048], P(('dp', 'expert')), may hold values from -6 to 6
- expert_ids: int32 [32768, 4], P(('dp', 'expert')), may hold values from 0 to 63, all different within a row; in each aligned block of 128 rows (0 to 127, 128 to 255, ...) at most 10 rows name the same one
- gate_probs: bfloat16 [32768, 4], P(('dp', 'expert')), may hold values from 0.049804688 to 1
- w_gate: bfloat16 [64, 2048, 512], P('expert', 'dp'), may hold values from -0.125 to 0.125
- w_up: bfloat16 [64, 2048, 512], P('expert', 'dp'), may hold values from -0.125 to 0.125
- w_down: bfloat16 [64, 512, 2048], P('expert', None, 'dp'), may hold values from -0.25 to 0.25
Outputs:
- mixed: bfloat16 [32768, 2048], P(('dp', 'expert'))
- grad_tokens: bfloat16 [32768, 2048], P(('dp', 'expert'))
- grad_gates: float32 [32768, 4], P(('dp', 'expert'))
- grad_gate_w: float32 [64, 2048, 512], P('expert', 'dp')
- grad_up_w: float32 [64, 2048, 512], P('expert', 'dp')
- grad_down_w: float32 [64, 512, 2048], P('expert', None, 'dp')
The draws below stay inside these ranges and needn't reach their ends.
Inputs may be any that keep to these rules, and one draw needn't show every extreme that they name: `expert_ids`: each row names 4 different experts. Within the rows of one device (aligned blocks of 128 rows) no expert is named by more than 10 rows, a bound that some block reaches.
All inputs are finite; a program needn't handle non-finite values.
Results may differ from the reference program's by a relative error of at most 0.0085.
Values may be sent and summed in bfloat16 or wider, within the bound.
No kernel may reach another device: no remote copies, remote signals or barrier semaphores. Data moves between devices by JAX's collectives and lax.ppermute only.
A program may use at most 128 MiB of HBM per device.

```python
import math
import jax
import jax.numpy as jnp
import numpy as np
from jax import lax

D = 2048
FW = 512
TOPK = 4
TOK_DEV = 128
EXPERTS = 64
TOKENS = 32768
CAP = 10
N_DP = 4
N_EXPERT = 64


def steps_of(key, shape, pieces, smallest, top_value):
    gain, own = 1.0, jax.random.fold_in(key, 6)
    for dim, shards_of in pieces:
        draws = jnp.exp(jax.random.uniform(jax.random.fold_in(own, dim), (shards_of,), jnp.float32, smallest / len(pieces), top_value / len(pieces)))
        gain = gain * jnp.repeat(draws, shape[dim] // shards_of).reshape([-1 if axis == dim else 1 for axis in range(len(shape))])
    return gain


def routed_block(stream_key, own, number, rows, amount, top, bound, skew):
    sequence = jax.random.permutation(stream_key, amount)
    heavy_load, ordinary = portions_of(amount, rows * top, bound, skew, True), portions_of(amount, rows * top, bound, skew, False)
    places = jnp.arange(amount)

    def named(sizes, offset_by):
        used = int((sizes > 0).sum())
        fixed = max(1, used // 4)
        passed = fixed + (places - fixed + offset_by * (used - fixed)) % max(1, amount - fixed)
        return jnp.zeros((amount,), jnp.int32).at[sequence[jnp.where(places < fixed, places, passed)]].set(jnp.asarray(sizes, jnp.int32))

    sizes = jnp.where(number % 4 == 0, named(heavy_load, number // 4), named(ordinary, number - number // 4 - 1))
    mixed = jax.random.permutation(jax.random.fold_in(own, 3), amount)
    donor, sink = mixed[0:amount // 2 * 2:2], mixed[1:amount // 2 * 2:2]
    slack = jnp.minimum(sizes[donor] - 1, bound - sizes[sink]) // 2
    slack = jnp.where((donor == sequence[0]) | (sink == sequence[0]) | (sizes[sink] == 0), 0, jnp.maximum(slack, 0))
    passed = jax.random.randint(jax.random.fold_in(own, 4), (amount // 2,), 0, 1 << 20) % (slack + 1)
    sizes = sizes.at[donor].add(-passed).at[sink].add(passed)
    members = jnp.searchsorted(jnp.cumsum(sizes), jnp.arange(rows * top), side="right").astype(jnp.int32)
    listing = members.reshape(top, rows).T
    listing = listing[jax.random.permutation(jax.random.fold_in(own, 1), rows)]
    offset_by = jax.random.randint(jax.random.fold_in(own, 2), (rows, 1), 0, top)
    return jnp.take_along_axis(listing, (jnp.arange(top)[None, :] + offset_by) % top, axis=1)


def portions_of(count, total, reach, lean, full):
    weights = [(1 << 20) // math.isqrt(standing ** lean) + 1 for standing in range(1, count + 1)]
    largest = reach if full else min(reach, max(-(-total // count), total * weights[0] // sum(weights)))
    least = 1 if total - largest >= count - 1 else 0
    counts, surplus = [largest] + [least] * (count - 1), total - largest - least * (count - 1)
    while surplus > 0:
        movable = [i for i in range(1, count) if counts[i] < largest] or [i for i in range(1, count) if counts[i] < reach]
        mass, remaining = sum([weights[i] for i in movable]), surplus
        for i in movable:
            extra = min(reach - counts[i], max(1, remaining * weights[i] // mass), surplus)
            counts[i] = counts[i] + extra
            surplus = surplus - extra
    return np.array(counts)


def noise(rng, dims, deviation, bound, pieces=(), kind=jnp.bfloat16):
    loudness = steps_of(rng, dims, pieces, -0.22, 0.18) if pieces else 1.0
    drawn = jax.random.normal(rng, dims, jnp.float32) * deviation * loudness
    return jnp.minimum(jnp.maximum(drawn, -bound), bound).astype(kind)


def setup_inputs(seed: int = 0) -> dict:
    key_list = jax.random.split(jax.random.key(seed), 8)
    tokens = noise(key_list[0], (TOKENS, D), 1.0, 6.0, ((0, 256),))
    cotangent = noise(key_list[1], (TOKENS, D), 1.0, 6.0, ((0, 256),))
    expert_ids_keys = jax.random.split(jax.random.fold_in(key_list[2], 1), TOKENS // TOK_DEV)
    expert_ids_turns = jax.random.permutation(jax.random.fold_in(key_list[2], 3), TOKENS // TOK_DEV)
    expert_ids = jax.vmap(lambda own, number: routed_block(jax.random.fold_in(key_list[2], 2), own, number, TOK_DEV, EXPERTS, TOPK, CAP, 2))(expert_ids_keys, expert_ids_turns).reshape((TOKENS, TOPK))
    gate_probs = jnp.clip(jnp.exp(math.log(1.0) - 2.9996462 * jax.random.uniform(key_list[3], (TOKENS, TOPK), jnp.float32) ** steps_of(key_list[3], (TOKENS, TOPK), ((0, 256),), -0.2, 0.2)), 0.049804688, 1.0).astype(jnp.bfloat16)
    w_gate = noise(key_list[4], (EXPERTS, D, FW), D ** -0.5, 0.125, ((0, 64), (1, 4)))
    w_up = noise(key_list[5], (EXPERTS, D, FW), D ** -0.5, 0.125, ((0, 64), (1, 4)))
    w_down = noise(key_list[6], (EXPERTS, FW, D), FW ** -0.5, 0.25, ((0, 64), (2, 4)))
    return {"tokens": tokens, "cotangent": cotangent, "expert_ids": expert_ids, "gate_probs": gate_probs, "w_gate": w_gate, "w_up": w_up, "w_down": w_down}


def silu_parts(pre_gate):
    sigma = jax.nn.sigmoid(pre_gate)
    return pre_gate * sigma, sigma * (1.0 + pre_gate * (1.0 - sigma))


def settle(partials):
    rounded = lax.optimization_barrier(partials.astype(jnp.bfloat16))
    return jnp.sum(rounded.astype(jnp.float32), axis=0)


def place_block(table_row, positions, values):
    return table_row.at[positions].set(values)


def reference(tokens, cotangent, expert_ids, gate_probs, w_gate, w_up, w_down):
    blocks = N_DP * N_EXPERT
    per_block = TOK_DEV * TOPK
    ids = expert_ids.reshape(blocks, per_block).astype(jnp.int32)
    onehot = (ids[:, :, None] == jnp.arange(EXPERTS, dtype=jnp.int32)[None, None, :]).astype(jnp.int32)
    earlier = jnp.cumsum(onehot, axis=1) - onehot
    slot_rank = jnp.sum(earlier * onehot, axis=2).astype(jnp.int32)
    position = (ids * CAP + slot_rank).astype(jnp.int32)
    pair_index = jnp.arange(blocks * per_block, dtype=jnp.int32).reshape(blocks, per_block)
    sentinel = TOKENS * TOPK
    table = jnp.full((blocks, EXPERTS * CAP), sentinel, jnp.int32)
    table = jax.vmap(place_block)(table, position, pair_index)
    table = table.reshape(blocks, EXPERTS, CAP).transpose(1, 0, 2).reshape(EXPERTS, N_DP, N_EXPERT * CAP)
    gate_flat = gate_probs.reshape(-1).astype(jnp.float32)

    def expert_pass(carry, inputs):
        mixed_acc, grad_acc, gates_acc = carry
        pairs, gate_w, up_w, down_w = inputs
        tok_index = (pairs // TOPK).astype(jnp.int32)
        rows_in = jnp.take(tokens, tok_index, axis=0, mode="fill", fill_value=0).astype(jnp.float32)
        cot_rows = jnp.take(cotangent, tok_index, axis=0, mode="fill", fill_value=0).astype(jnp.float32)
        weights = jnp.take(gate_flat, pairs, axis=0, mode="fill", fill_value=0)
        routed = (weights[:, :, None] * cot_rows).astype(jnp.bfloat16).astype(jnp.float32)
        gate_f = gate_w.astype(jnp.float32)
        up_f = up_w.astype(jnp.float32)
        down_f = down_w.astype(jnp.float32)
        pre_gate = jnp.einsum("qnd,df->qnf", rows_in, gate_f)
        pre_up = jnp.einsum("qnd,df->qnf", rows_in, up_f)
        activated, slope = silu_parts(pre_gate)
        hidden = (activated * pre_up).astype(jnp.bfloat16).astype(jnp.float32)
        expert_out = jnp.einsum("qnf,fd->qnd", hidden, down_f).astype(jnp.bfloat16).astype(jnp.float32)
        grad_hidden = jnp.einsum("qnd,fd->qnf", routed, down_f)
        grad_pre_gate = (grad_hidden * pre_up * slope).astype(jnp.bfloat16).astype(jnp.float32)
        grad_pre_up = (grad_hidden * activated).astype(jnp.bfloat16).astype(jnp.float32)
        pair_grad = (jnp.einsum("qnf,df->qnd", grad_pre_gate, gate_f) + jnp.einsum("qnf,df->qnd", grad_pre_up, up_f)).astype(jnp.bfloat16).astype(jnp.float32)
        mixed_acc = mixed_acc.at[tok_index].add(weights[:, :, None] * expert_out, mode="drop")
        grad_acc = grad_acc.at[tok_index].add(pair_grad, mode="drop")
        gates_acc = gates_acc.at[pairs].add(jnp.sum(cot_rows * expert_out, axis=-1), mode="drop")
        grad_gate_e = settle(jnp.einsum("qnd,qnf->qdf", rows_in, grad_pre_gate))
        grad_up_e = settle(jnp.einsum("qnd,qnf->qdf", rows_in, grad_pre_up))
        grad_down_e = settle(jnp.einsum("qnf,qnd->qfd", hidden, routed))
        return (mixed_acc, grad_acc, gates_acc), (grad_gate_e, grad_up_e, grad_down_e)

    start = (jnp.zeros((TOKENS, D), jnp.float32), jnp.zeros((TOKENS, D), jnp.float32), jnp.zeros((TOKENS * TOPK,), jnp.float32))
    final, grads = lax.scan(expert_pass, start, (table, w_gate, w_up, w_down))
    mixed_acc, grad_acc, gates_acc = final
    return (mixed_acc.astype(jnp.bfloat16), grad_acc.astype(jnp.bfloat16), gates_acc.reshape(TOKENS, TOPK), grads[0], grads[1], grads[2])
```

```python
import functools

import jax
import jax.numpy as jnp
from jax import lax
from jax.experimental import pallas as pl
from jax.experimental.pallas import tpu as pltpu
from jax.sharding import PartitionSpec as P


INTERPRET = False
LANES = 128


def smem():
    return pl.BlockSpec(memory_space=pltpu.SMEM)


def vmem():
    return pl.BlockSpec(memory_space=pltpu.VMEM)


def clear_rows(out_ref, step=16):
    rows = out_ref.shape[0]
    zero = jnp.zeros((step,) + out_ref.shape[1:], out_ref.dtype)

    def body(i, carry):
        out_ref[pl.ds(i * step, step)] = zero
        return carry

    lax.fori_loop(0, rows // step, body, 0)


def route_kernel(top, capacity, ids_ref, tok_ref, out_ref, pos_ref, count_ref):
    def reset(i, carry):
        count_ref[i] = 0
        return carry

    lax.fori_loop(0, count_ref.shape[0], reset, 0)
    clear_rows(out_ref)

    def body(t, carry):
        row = tok_ref[t]
        names = [ids_ref[top * t + k] for k in range(top)]
        slots = [count_ref[e] for e in names]
        for k in range(top):
            count_ref[names[k]] = slots[k] + 1
            place = names[k] * capacity + slots[k]
            pos_ref[top * t + k] = place
            out_ref[place] = row
        return carry

    lax.fori_loop(0, tok_ref.shape[0], body, 0)


def weigh_kernel(top, pos_ref, gate_ref, cot_ref, out_ref):
    clear_rows(out_ref)

    def body(t, carry):
        row = cot_ref[t].astype(jnp.float32)
        for k in range(top):
            out_ref[pos_ref[top * t + k]] = (row * gate_ref[top * t + k]).astype(jnp.bfloat16)
        return carry

    lax.fori_loop(0, cot_ref.shape[0], body, 0)


def mix_kernel(top, pos_ref, gate_ref, cot_ref, back_ref, mixed_ref, dots_ref):
    def body(t, carry):
        cot = cot_ref[t].astype(jnp.float32)
        total = jnp.zeros(cot.shape, jnp.float32)
        for k in range(top):
            row = back_ref[pos_ref[top * t + k]].astype(jnp.float32)
            total = total + row * gate_ref[top * t + k]
            dots_ref[pl.ds(top * t + k, 1), :] = jnp.sum(row * cot, axis=0, keepdims=True)
        mixed_ref[t] = total.astype(jnp.bfloat16)
        return carry

    lax.fori_loop(0, cot_ref.shape[0], body, 0)


def gather_sum_kernel(top, pos_ref, back_ref, out_ref):
    def body(t, carry):
        total = back_ref[pos_ref[top * t]].astype(jnp.float32)
        for k in range(1, top):
            total = total + back_ref[pos_ref[top * t + k]].astype(jnp.float32)
        out_ref[t] = total.astype(jnp.bfloat16)
        return carry

    lax.fori_loop(0, out_ref.shape[0], body, 0)


def silu_parts(pre_gate):
    sigma = jax.nn.sigmoid(pre_gate)
    return (pre_gate * sigma, sigma * (1.0 + pre_gate * (1.0 - sigma)))


def to_rows(wire, width):
    return wire.reshape(-1, width)


def to_wire(rows, sublanes):
    return rows.reshape(-1, sublanes, LANES)


def on_device(tokens, cotangent, expert_ids, gate_probs, w_gate, w_up, w_down):
    group = lax.axis_size("expert")
    all_experts = w_gate.shape[0] * group
    rows, width = tokens.shape
    top = expert_ids.shape[1]
    capacity = max(2, 5 * rows * top // (4 * all_experts))
    slots = all_experts * capacity
    sub = width // LANES
    f32, bf16 = jnp.float32, jnp.bfloat16

    def exchange(x):
        chunks = x.reshape(group, capacity * sub, LANES)
        return lax.all_to_all(chunks, "expert", 0, 0, tiled=True).reshape(slots, sub, LANES)

    wire_shape = jax.ShapeDtypeStruct((slots, sub, LANES), bf16)
    token_shape = jax.ShapeDtypeStruct((rows, sub, LANES), bf16)
    params = pltpu.CompilerParams(vmem_limit_bytes=32 << 20)
    call = functools.partial(pl.pallas_call, compiler_params=params, interpret=INTERPRET)

    flat_ids = expert_ids.reshape(-1)
    gates = gate_probs.astype(f32).reshape(-1)
    token_tiles = to_wire(tokens, sub)
    cot_tiles = to_wire(cotangent, sub)

    token_send, position = call(
        functools.partial(route_kernel, top, capacity),
        out_shape=(wire_shape, jax.ShapeDtypeStruct((rows * top,), jnp.int32)),
        in_specs=[smem(), vmem()],
        out_specs=(vmem(), smem()),
        scratch_shapes=[pltpu.SMEM((all_experts,), jnp.int32)],
        name="route",
    )(flat_ids, token_tiles)
    token_recv = exchange(token_send)

    routed_send = call(
        functools.partial(weigh_kernel, top),
        out_shape=wire_shape,
        in_specs=[smem(), smem(), vmem()],
        out_specs=vmem(),
        name="weigh",
    )(position, gates, cot_tiles)
    routed_recv = exchange(routed_send)

    full_gate = lax.all_gather(w_gate[0], "dp", axis=0, tiled=True)
    full_up = lax.all_gather(w_up[0], "dp", axis=0, tiled=True)
    full_down = lax.all_gather(w_down[0], "dp", axis=1, tiled=True)

    def dot(a, b, dims):
        return lax.dot_general(a, b, (dims, ((), ())), preferred_element_type=f32)

    rows_in = to_rows(token_recv, width)
    pre_gate = dot(rows_in, full_gate, ((1,), (0,)))
    pre_up = dot(rows_in, full_up, ((1,), (0,)))
    activated, _ = silu_parts(pre_gate)
    hidden = (activated * pre_up).astype(bf16)
    expert_out = dot(hidden, full_down, ((1,), (0,))).astype(bf16)
    out_send = to_wire(expert_out, sub)
    back_out = exchange(out_send)

    routed_recv, pre_gate, pre_up, _ = lax.optimization_barrier(
        (routed_recv, pre_gate, pre_up, out_send)
    )
    activated, slope = silu_parts(pre_gate)
    routed_in = to_rows(routed_recv, width)
    grad_hidden = dot(routed_in, full_down, ((1,), (1,)))
    grad_pre_gate = (grad_hidden * pre_up * slope).astype(bf16)
    grad_pre_up = (grad_hidden * activated).astype(bf16)
    pair_grad = dot(grad_pre_gate, full_gate, ((1,), (1,)))
    pair_grad = (pair_grad + dot(grad_pre_up, full_up, ((1,), (1,)))).astype(bf16)
    grad_send = to_wire(pair_grad, sub)
    back_grad = exchange(grad_send)

    def weight_part(a, b):
        return dot(a, b, ((0,), (0,))).astype(bf16)

    def reduce_weight(part, axis):
        return lax.psum_scatter(part, "dp", scatter_dimension=axis, tiled=True).astype(f32)[None]

    grad_down_w = reduce_weight(weight_part(hidden, routed_in), 1)
    grad_gate_w = reduce_weight(weight_part(rows_in, grad_pre_gate), 0)
    grad_up_w = reduce_weight(weight_part(rows_in, grad_pre_up), 0)

    mixed, dots = call(
        functools.partial(mix_kernel, top),
        out_shape=(token_shape, jax.ShapeDtypeStruct((rows * top, LANES), f32)),
        in_specs=[smem(), smem(), vmem(), vmem()],
        out_specs=(vmem(), vmem()),
        name="mix",
    )(position, gates, cot_tiles, back_out)
    grad_gates = jnp.sum(dots, axis=1).reshape(rows, top)

    grad_tokens = call(
        functools.partial(gather_sum_kernel, top),
        out_shape=token_shape,
        in_specs=[smem(), vmem()],
        out_specs=vmem(),
        name="gather_sum",
    )(position, back_grad)
    return (
        to_rows(mixed, width),
        to_rows(grad_tokens, width),
        grad_gates,
        grad_gate_w,
        grad_up_w,
        grad_down_w,
    )


def solution(mesh):
    tokens = P(("dp", "expert"), None)
    first = P("expert", "dp", None)
    last = P("expert", None, "dp")

    return jax.shard_map(
        on_device,
        mesh=mesh,
        in_specs=(tokens, tokens, tokens, tokens, first, first, last),
        out_specs=(tokens, tokens, tokens, first, first, last),
        check_vma=False,
    )
```

```python
import functools

import jax
import jax.numpy as jnp
from jax import lax
from jax.experimental import pallas as pl
from jax.experimental.pallas import tpu as pltpu
from jax.sharding import PartitionSpec as P


INTERPRET = False
LANES = 128


def smem():
    return pl.BlockSpec(memory_space=pltpu.SMEM)


def vmem():
    return pl.BlockSpec(memory_space=pltpu.VMEM)


def clear_rows(out_ref, step=16):
    rows = out_ref.shape[0]
    zero = jnp.zeros((step,) + out_ref.shape[1:], out_ref.dtype)

    def body(i, carry):
        out_ref[pl.ds(i * step, step)] = zero
        return carry

    lax.fori_loop(0, rows // step, body, 0)


def route_kernel(top, capacity, ids_ref, tok_ref, out_ref, pos_ref, count_ref):
    def reset(i, carry):
        count_ref[i] = 0
        return carry

    lax.fori_loop(0, count_ref.shape[0], reset, 0)
    clear_rows(out_ref)

    def body(t, carry):
        row = tok_ref[t]
        names = [ids_ref[k, t] for k in range(top)]
        slots = [count_ref[e] for e in names]
        for k in range(top):
            count_ref[names[k]] = slots[k] + 1
            place = names[k] * capacity + slots[k]
            pos_ref[k, t] = place
            out_ref[place] = row
        return carry

    lax.fori_loop(0, tok_ref.shape[0], body, 0)


def weigh_kernel(top, pos_ref, gate_ref, cot_ref, out_ref):
    clear_rows(out_ref)

    def body(t, carry):
        row = cot_ref[t].astype(jnp.float32)
        for k in range(top):
            out_ref[pos_ref[k, t]] = (row * gate_ref[k, t]).astype(jnp.bfloat16)
        return carry

    lax.fori_loop(0, cot_ref.shape[0], body, 0)


def mix_kernel(top, pos_ref, gate_ref, cot_ref, back_ref, mixed_ref, dots_ref):
    rows = cot_ref.shape[0]

    def body(t, carry):
        cot = cot_ref[t].astype(jnp.float32)
        total = jnp.zeros(cot.shape, jnp.float32)
        for k in range(top):
            row = back_ref[pos_ref[k, t]].astype(jnp.float32)
            total = total + row * gate_ref[k, t]
            dots_ref[pl.ds(k * rows + t, 1), :] = jnp.sum(row * cot, axis=0, keepdims=True)
        mixed_ref[t] = total.astype(jnp.bfloat16)
        return carry

    lax.fori_loop(0, cot_ref.shape[0], body, 0)


def gather_sum_kernel(top, pos_ref, back_ref, out_ref):
    def body(t, carry):
        total = back_ref[pos_ref[0, t]].astype(jnp.float32)
        for k in range(1, top):
            total = total + back_ref[pos_ref[k, t]].astype(jnp.float32)
        out_ref[t] = total.astype(jnp.bfloat16)
        return carry

    lax.fori_loop(0, out_ref.shape[0], body, 0)


def silu_parts(pre_gate):
    sigma = jax.nn.sigmoid(pre_gate)
    return (pre_gate * sigma, sigma * (1.0 + pre_gate * (1.0 - sigma)))


def to_rows(wire, width):
    return wire.reshape(-1, width)


def to_wire(rows, sublanes):
    return rows.reshape(-1, sublanes, LANES)


def on_device(tokens, cotangent, expert_ids, gate_probs, w_gate, w_up, w_down):
    group = lax.axis_size("expert")
    all_experts = w_gate.shape[0] * group
    rows, width = tokens.shape
    top = expert_ids.shape[1]
    capacity = max(2, 5 * rows * top // (4 * all_experts))
    slots = all_experts * capacity
    sub = width // LANES
    f32, bf16 = jnp.float32, jnp.bfloat16

    def exchange(x):
        chunks = x.reshape(group, capacity * sub, LANES)
        return lax.all_to_all(chunks, "expert", 0, 0, tiled=True).reshape(slots, sub, LANES)

    wire_shape = jax.ShapeDtypeStruct((slots, sub, LANES), bf16)
    token_shape = jax.ShapeDtypeStruct((rows, sub, LANES), bf16)
    params = pltpu.CompilerParams(vmem_limit_bytes=32 << 20)
    call = functools.partial(pl.pallas_call, compiler_params=params, interpret=INTERPRET)

    gates = gate_probs.T.astype(f32)
    token_tiles = to_wire(tokens, sub)
    cot_tiles = to_wire(cotangent, sub)

    token_send, position = call(
        functools.partial(route_kernel, top, capacity),
        out_shape=(wire_shape, jax.ShapeDtypeStruct((top, rows), jnp.int32)),
        in_specs=[smem(), vmem()],
        out_specs=(vmem(), smem()),
        scratch_shapes=[pltpu.SMEM((all_experts,), jnp.int32)],
        name="route",
    )(expert_ids.T, token_tiles)
    token_recv = exchange(token_send)

    routed_send = call(
        functools.partial(weigh_kernel, top),
        out_shape=wire_shape,
        in_specs=[smem(), smem(), vmem()],
        out_specs=vmem(),
        name="weigh",
    )(position, gates, cot_tiles)
    routed_recv = exchange(routed_send)

    replicas = lax.axis_size("dp")
    here = lax.axis_index("dp")

    def to_replica(x, step):
        return lax.ppermute(x, "dp", [(i, (i + step) % replicas) for i in range(replicas)])

    def gather_replicas(shard, axis):
        size = shard.shape[axis]
        shape = list(shard.shape)
        shape[axis] = size * replicas
        full = jnp.zeros(shape, shard.dtype)
        for step in range(replicas):
            piece = to_replica(shard, step) if step else shard
            place = (here - step) % replicas * size
            full = lax.dynamic_update_slice_in_dim(full, piece, place, axis)
        return full

    def sum_replicas(part, axis):
        size = part.shape[axis] // replicas
        total = None
        for step in range(replicas):
            place = (here + step) % replicas * size
            piece = lax.dynamic_slice_in_dim(part, place, size, axis)
            piece = to_replica(piece, step) if step else piece
            piece = piece.astype(f32)
            total = piece if total is None else total + piece
        return total

    hid = w_gate.shape[2]
    full_in = gather_replicas(jnp.concatenate([w_gate[0], w_up[0]], axis=1), 0)
    full_down = gather_replicas(w_down[0], 1)

    def dot(a, b, dims):
        return lax.dot_general(a, b, (dims, ((), ())), preferred_element_type=f32)

    rows_in = to_rows(token_recv, width)
    pre = dot(rows_in, full_in, ((1,), (0,)))
    pre_gate, pre_up = pre[:, :hid], pre[:, hid:]
    activated, _ = silu_parts(pre_gate)
    hidden = (activated * pre_up).astype(bf16)
    expert_out = dot(hidden, full_down, ((1,), (0,))).astype(bf16)
    out_send = to_wire(expert_out, sub)
    back_out = exchange(out_send)

    routed_recv, pre, _ = lax.optimization_barrier((routed_recv, pre, out_send))
    pre_gate, pre_up = pre[:, :hid], pre[:, hid:]
    activated, slope = silu_parts(pre_gate)
    routed_in = to_rows(routed_recv, width)
    grad_hidden = dot(routed_in, full_down, ((1,), (1,)))
    grad_pre = jnp.concatenate(
        [
            (grad_hidden * pre_up * slope).astype(bf16),
            (grad_hidden * activated).astype(bf16),
        ],
        axis=1,
    )
    pair_grad = dot(grad_pre, full_in, ((1,), (1,))).astype(bf16)
    grad_send = to_wire(pair_grad, sub)
    back_grad = exchange(grad_send)

    def weight_part(a, b):
        return dot(a, b, ((0,), (0,))).astype(bf16)

    grad_down_w = sum_replicas(weight_part(hidden, routed_in), 1)[None]
    grad_in = sum_replicas(weight_part(rows_in, grad_pre), 0)
    grad_gate_w, grad_up_w = grad_in[None, :, :hid], grad_in[None, :, hid:]

    mixed, dots = call(
        functools.partial(mix_kernel, top),
        out_shape=(token_shape, jax.ShapeDtypeStruct((rows * top, LANES), f32)),
        in_specs=[smem(), smem(), vmem(), vmem()],
        out_specs=(vmem(), vmem()),
        name="mix",
    )(position, gates, cot_tiles, back_out)
    grad_gates = jnp.sum(dots, axis=1).reshape(top, rows).T

    grad_tokens = call(
        functools.partial(gather_sum_kernel, top),
        out_shape=token_shape,
        in_specs=[smem(), vmem()],
        out_specs=vmem(),
        name="gather_sum",
    )(position, back_grad)
    return (
        to_rows(mixed, width),
        to_rows(grad_tokens, width),
        grad_gates,
        grad_gate_w,
        grad_up_w,
        grad_down_w,
    )


def solution(mesh):
    tokens = P(("dp", "expert"), None)
    first = P("expert", "dp", None)
    last = P("expert", None, "dp")

    return jax.shard_map(
        on_device,
        mesh=mesh,
        in_specs=(tokens, tokens, tokens, tokens, first, first, last),
        out_specs=(tokens, tokens, tokens, first, first, last),
        check_vma=False,
    )
```

```python
import functools

import jax
import jax.numpy as jnp
from jax import lax
from jax.experimental import pallas as pl
from jax.experimental.pallas import tpu as pltpu
from jax.sharding import PartitionSpec as P


INTERPRET = False
LANES = 128
CORES = 2


def smem():
    return pl.BlockSpec(memory_space=pltpu.SMEM)


def vmem():
    return pl.BlockSpec(memory_space=pltpu.VMEM)


def clear_rows(out_ref, step=16):
    rows = out_ref.shape[0]
    zero = jnp.zeros((step,) + out_ref.shape[1:], out_ref.dtype)

    def body(i, carry):
        out_ref[pl.ds(i * step, step)] = zero
        return carry

    lax.fori_loop(0, rows // step, body, 0)


def for_each(count, body, unroll=4):
    def step(i, carry):
        for j in range(unroll):
            body(unroll * i + j)
        return carry

    lax.fori_loop(0, count // unroll, step, 0)


def route_kernel(top, capacity, ids_ref, tok_ref, out_ref, pos_ref, count_ref):
    def reset(i, carry):
        count_ref[i] = 0
        return carry

    lax.fori_loop(0, count_ref.shape[0], reset, 0)
    clear_rows(out_ref)

    def body(t):
        row = tok_ref[t]
        names = [ids_ref[k, t] for k in range(top)]
        slots = [count_ref[e] for e in names]
        for k in range(top):
            count_ref[names[k]] = slots[k] + 1
            place = names[k] * capacity + slots[k]
            pos_ref[k, t] = place
            out_ref[place] = row

    for_each(tok_ref.shape[0], body)


def weigh_kernel(top, pos_ref, gate_ref, cot_ref, keep_ref, give_ref, all_ref):
    half = keep_ref.shape[0]
    clear_rows(all_ref)

    def body(t):
        row = cot_ref[t].astype(jnp.float32)
        for k in range(top):
            all_ref[pos_ref[k, t]] = (row * gate_ref[k, t]).astype(jnp.bfloat16)

    for_each(cot_ref.shape[0], body, 2)

    def part(i):
        keep_ref[i] = all_ref[i]
        give_ref[i] = all_ref[half + i]

    for_each(half, part)


def pack_kernel(capacity, core_ref, keep_ref, got_ref, *out_refs):
    mine = core_ref[0] * capacity
    other = capacity - mine
    for d, out_ref in enumerate(out_refs):
        out_ref[pl.ds(mine, capacity)] = keep_ref[pl.ds(d * capacity, capacity)]
        out_ref[pl.ds(other, capacity)] = got_ref[pl.ds(d * capacity, capacity)]


def place_kernel(chip_ref, *refs):
    block_refs, out_ref = refs[:-1], refs[-1]
    chips, size = len(block_refs), block_refs[0].shape[0]
    for d, block_ref in enumerate(block_refs):
        source = chip_ref[0] - d
        source = jnp.where(source < 0, source + chips, source)
        out_ref[pl.ds(source * size, size)] = block_ref[...]


def mix_kernel(top, pos_ref, gate_ref, cot_ref, back_ref, mixed_ref, dots_ref):
    rows = cot_ref.shape[0]

    def body(t, carry):
        cot = cot_ref[t].astype(jnp.float32)
        total = jnp.zeros(cot.shape, jnp.float32)
        for k in range(top):
            row = back_ref[pos_ref[k, t]].astype(jnp.float32)
            total = total + row * gate_ref[k, t]
            dots_ref[pl.ds(k * rows + t, 1), :] = jnp.sum(row * cot, axis=0, keepdims=True)
        mixed_ref[t] = total.astype(jnp.bfloat16)
        return carry

    lax.fori_loop(0, cot_ref.shape[0], body, 0)


def gather_sum_kernel(top, pos_ref, back_ref, out_ref):
    def body(t):
        total = back_ref[pos_ref[0, t]].astype(jnp.float32)
        for k in range(1, top):
            total = total + back_ref[pos_ref[k, t]].astype(jnp.float32)
        out_ref[t] = total.astype(jnp.bfloat16)

    for_each(out_ref.shape[0], body)


def silu_parts(pre_gate):
    sigma = jax.nn.sigmoid(pre_gate)
    return (pre_gate * sigma, sigma * (1.0 + pre_gate * (1.0 - sigma)))


def to_rows(wire, width):
    return wire.reshape(-1, width)


def to_wire(rows, sublanes):
    return rows.reshape(-1, sublanes, LANES)


def on_device(tokens, cotangent, expert_ids, gate_probs, w_gate, w_up, w_down):
    group = lax.axis_size("expert")
    all_experts = w_gate.shape[0] * group
    rows, width = tokens.shape
    top = expert_ids.shape[1]
    capacity = max(2, 5 * rows * top // (4 * all_experts))
    slots = all_experts * capacity
    sub = width // LANES
    f32, bf16 = jnp.float32, jnp.bfloat16

    def exchange(x):
        chunks = x.reshape(group, capacity * sub, LANES)
        return lax.all_to_all(chunks, "expert", 0, 0, tiled=True).reshape(slots, sub, LANES)

    wire_shape = jax.ShapeDtypeStruct((slots, sub, LANES), bf16)
    token_shape = jax.ShapeDtypeStruct((rows, sub, LANES), bf16)
    params = pltpu.CompilerParams(vmem_limit_bytes=32 << 20)
    call = functools.partial(pl.pallas_call, compiler_params=params, interpret=INTERPRET)

    gates = gate_probs.T.astype(f32)
    token_tiles = to_wire(tokens, sub)
    cot_tiles = to_wire(cotangent, sub)

    token_send, position = call(
        functools.partial(route_kernel, top, capacity),
        out_shape=(wire_shape, jax.ShapeDtypeStruct((top, rows), jnp.int32)),
        in_specs=[smem(), vmem()],
        out_specs=(vmem(), smem()),
        scratch_shapes=[pltpu.SMEM((all_experts,), jnp.int32)],
        name="route",
    )(expert_ids.T, token_tiles)
    token_recv = exchange(token_send)

    chips = group // CORES
    device = lax.axis_index("expert")
    chip, core = device // CORES, device % CORES
    name, slot = position // capacity, position % capacity
    leap = (name // CORES - chip) % chips
    rank = ((name % CORES + core) % CORES * chips + leap) * capacity + slot
    half = jax.ShapeDtypeStruct((chips * capacity, sub, LANES), bf16)
    block = jax.ShapeDtypeStruct((CORES * capacity, sub, LANES), bf16)
    keep, give = call(
        functools.partial(weigh_kernel, top),
        out_shape=(half, half),
        in_specs=[smem(), smem(), vmem()],
        out_specs=(vmem(), vmem()),
        scratch_shapes=[pltpu.VMEM((slots, sub, LANES), bf16)],
        name="weigh",
    )(rank, gates, cot_tiles)
    got = lax.ppermute(give, "expert", [(i, i ^ 1) for i in range(group)])
    blocks = call(
        functools.partial(pack_kernel, capacity),
        out_shape=(block,) * chips,
        in_specs=[smem(), vmem(), vmem()],
        out_specs=(vmem(),) * chips,
        name="pack",
    )(core.reshape(1), keep, got)
    arrived = [blocks[0]] + [
        lax.ppermute(
            blocks[d],
            "expert",
            [(i, (i + CORES * d) % group) for i in range(group)],
        )
        for d in range(1, chips)
    ]

    replicas = lax.axis_size("dp")
    here = lax.axis_index("dp")

    def to_replica(x, step):
        return lax.ppermute(x, "dp", [(i, (i + step) % replicas) for i in range(replicas)])

    def gather_replicas(shard, axis):
        size = shard.shape[axis]
        shape = list(shard.shape)
        shape[axis] = size * replicas
        full = jnp.zeros(shape, shard.dtype)
        for step in range(replicas):
            piece = to_replica(shard, step) if step else shard
            place = (here - step) % replicas * size
            full = lax.dynamic_update_slice_in_dim(full, piece, place, axis)
        return full

    def sum_replicas(part, axis):
        size = part.shape[axis] // replicas
        total = None
        for step in range(replicas):
            place = (here + step) % replicas * size
            piece = lax.dynamic_slice_in_dim(part, place, size, axis)
            piece = to_replica(piece, step) if step else piece
            piece = piece.astype(f32)
            total = piece if total is None else total + piece
        return total

    hid = w_gate.shape[2]
    full_in = gather_replicas(jnp.concatenate([w_gate[0], w_up[0]], axis=1), 0)
    full_down = gather_replicas(w_down[0], 1)

    def dot(a, b, dims):
        return lax.dot_general(a, b, (dims, ((), ())), preferred_element_type=f32)

    rows_in = to_rows(token_recv, width)
    pre = dot(rows_in, full_in, ((1,), (0,)))
    pre_gate, pre_up = pre[:, :hid], pre[:, hid:]
    activated, _ = silu_parts(pre_gate)
    hidden = (activated * pre_up).astype(bf16)
    expert_out = dot(hidden, full_down, ((1,), (0,))).astype(bf16)
    out_send = to_wire(expert_out, sub)
    back_out = exchange(out_send)

    arrived, pre, _ = lax.optimization_barrier((arrived, pre, out_send))
    pre_gate, pre_up = pre[:, :hid], pre[:, hid:]
    activated, slope = silu_parts(pre_gate)
    routed_recv = call(
        place_kernel,
        out_shape=wire_shape,
        in_specs=[smem()] + [vmem()] * chips,
        out_specs=vmem(),
        name="place",
    )(chip.reshape(1), *arrived)
    routed_in = to_rows(routed_recv, width)
    grad_hidden = dot(routed_in, full_down, ((1,), (1,)))
    grad_pre = jnp.concatenate(
        [
            (grad_hidden * pre_up * slope).astype(bf16),
            (grad_hidden * activated).astype(bf16),
        ],
        axis=1,
    )
    pair_grad = dot(grad_pre, full_in, ((1,), (1,))).astype(bf16)
    grad_send = to_wire(pair_grad, sub)
    back_grad = exchange(grad_send)

    def weight_part(a, b):
        return dot(a, b, ((0,), (0,))).astype(bf16)

    grad_down_w = sum_replicas(weight_part(hidden, routed_in), 1)[None]
    grad_in = sum_replicas(weight_part(rows_in, grad_pre), 0)
    grad_gate_w, grad_up_w = grad_in[None, :, :hid], grad_in[None, :, hid:]

    mixed, dots = call(
        functools.partial(mix_kernel, top),
        out_shape=(token_shape, jax.ShapeDtypeStruct((rows * top, LANES), f32)),
        in_specs=[smem(), smem(), vmem(), vmem()],
        out_specs=(vmem(), vmem()),
        name="mix",
    )(position, gates, cot_tiles, back_out)
    grad_gates = jnp.sum(dots, axis=1).reshape(top, rows).T

    grad_tokens = call(
        functools.partial(gather_sum_kernel, top),
        out_shape=token_shape,
        in_specs=[smem(), vmem()],
        out_specs=vmem(),
        name="gather_sum",
    )(position, back_grad)
    return (
        to_rows(mixed, width),
        to_rows(grad_tokens, width),
        grad_gates,
        grad_gate_w,
        grad_up_w,
        grad_down_w,
    )


def solution(mesh):
    tokens = P(("dp", "expert"), None)
    first = P("expert", "dp", None)
    last = P("expert", None, "dp")

    return jax.shard_map(
        on_device,
        mesh=mesh,
        in_specs=(tokens, tokens, tokens, tokens, first, first, last),
        out_specs=(tokens, tokens, tokens, first, first, last),
        check_vma=False,
    )
```

```python
import functools

import jax
import jax.numpy as jnp
from jax import lax
from jax.experimental import pallas as pl
from jax.experimental.pallas import tpu as pltpu
from jax.sharding import PartitionSpec as P


INTERPRET = False
LANES = 128


def smem():
    return pl.BlockSpec(memory_space=pltpu.SMEM)


def vmem():
    return pl.BlockSpec(memory_space=pltpu.VMEM)


def clear_rows(out_ref, step=16):
    rows = out_ref.shape[0]
    zero = jnp.zeros((step,) + out_ref.shape[1:], out_ref.dtype)

    def body(i, carry):
        out_ref[pl.ds(i * step, step)] = zero
        return carry

    lax.fori_loop(0, rows // step, body, 0)


def for_each(count, body, unroll=4):
    def step(i, carry):
        for j in range(unroll):
            body(unroll * i + j)
        return carry

    lax.fori_loop(0, count // unroll, step, 0)


def route_kernel(capacity, experts, ids_ref, tok_ref, out_ref, pos_ref, place_ref, sem):
    top, rows = ids_ref.shape
    f32 = jnp.float32
    expert = lax.broadcasted_iota(jnp.int32, (experts, rows), 0)
    hits = [ids_ref[pl.ds(k, 1), :] == expert for k in range(top)]
    named = sum(hit.astype(f32) for hit in hits).astype(jnp.bfloat16)
    first = lax.broadcasted_iota(jnp.int32, (rows, rows), 0)
    second = lax.broadcasted_iota(jnp.int32, (rows, rows), 1)
    before = (first < second).astype(f32).astype(jnp.bfloat16)
    rank = jnp.dot(named, before, preferred_element_type=f32)
    slot = (expert * capacity).astype(f32) + rank
    for k in range(top):
        chosen = jnp.sum(jnp.where(hits[k], slot, 0.0), axis=0, keepdims=True)
        pos_ref[pl.ds(k, 1), :] = chosen.astype(jnp.int32)
    copy = pltpu.make_async_copy(pos_ref, place_ref, sem)
    copy.start()
    clear_rows(out_ref)
    copy.wait()

    def body(t):
        row = tok_ref[t]
        for k in range(top):
            out_ref[place_ref[k, t]] = row

    for_each(rows, body)


def weigh_kernel(top, pos_ref, gate_ref, cot_ref, out_ref):
    clear_rows(out_ref)

    def body(t, carry):
        row = cot_ref[t].astype(jnp.float32)
        for k in range(top):
            out_ref[pos_ref[k, t]] = (row * gate_ref[k, t]).astype(jnp.bfloat16)
        return carry

    lax.fori_loop(0, cot_ref.shape[0], body, 0)


def mix_kernel(top, pos_ref, gate_ref, cot_ref, back_ref, mixed_ref, dots_ref):
    rows = cot_ref.shape[0]

    def body(t, carry):
        cot = cot_ref[t].astype(jnp.float32)
        total = jnp.zeros(cot.shape, jnp.float32)
        for k in range(top):
            row = back_ref[pos_ref[k, t]].astype(jnp.float32)
            total = total + row * gate_ref[k, t]
            dots_ref[pl.ds(k * rows + t, 1), :] = jnp.sum(row * cot, axis=0, keepdims=True)
        mixed_ref[t] = total.astype(jnp.bfloat16)
        return carry

    lax.fori_loop(0, cot_ref.shape[0], body, 0)


def gather_sum_kernel(top, pos_ref, back_ref, out_ref):
    def body(t):
        total = back_ref[pos_ref[0, t]].astype(jnp.float32)
        for k in range(1, top):
            total = total + back_ref[pos_ref[k, t]].astype(jnp.float32)
        out_ref[t] = total.astype(jnp.bfloat16)

    for_each(out_ref.shape[0], body, 8)


def silu_parts(pre_gate):
    sigma = jax.nn.sigmoid(pre_gate)
    return (pre_gate * sigma, sigma * (1.0 + pre_gate * (1.0 - sigma)))


def to_rows(wire, width):
    return wire.reshape(-1, width)


def to_wire(rows, sublanes):
    return rows.reshape(-1, sublanes, LANES)


def on_device(tokens, cotangent, expert_ids, gate_probs, w_gate, w_up, w_down):
    group = lax.axis_size("expert")
    all_experts = w_gate.shape[0] * group
    rows, width = tokens.shape
    top = expert_ids.shape[1]
    capacity = max(2, 5 * rows * top // (4 * all_experts))
    slots = all_experts * capacity
    sub = width // LANES
    f32, bf16 = jnp.float32, jnp.bfloat16

    def exchange(x):
        chunks = x.reshape(group, capacity * sub, LANES)
        return lax.all_to_all(chunks, "expert", 0, 0, tiled=True).reshape(slots, sub, LANES)

    wire_shape = jax.ShapeDtypeStruct((slots, sub, LANES), bf16)
    token_shape = jax.ShapeDtypeStruct((rows, sub, LANES), bf16)
    params = pltpu.CompilerParams(vmem_limit_bytes=32 << 20)
    call = functools.partial(pl.pallas_call, compiler_params=params, interpret=INTERPRET)

    gates = gate_probs.T.astype(f32)
    token_tiles = to_wire(tokens, sub)
    cot_tiles = to_wire(cotangent, sub)

    token_send, position = call(
        functools.partial(route_kernel, capacity, all_experts),
        out_shape=(wire_shape, jax.ShapeDtypeStruct((top, rows), jnp.int32)),
        in_specs=[vmem(), vmem()],
        out_specs=(vmem(), vmem()),
        scratch_shapes=[pltpu.SMEM((top, rows), jnp.int32), pltpu.SemaphoreType.DMA],
        name="route",
    )(expert_ids.T, token_tiles)
    token_recv = exchange(token_send)

    routed_send = call(
        functools.partial(weigh_kernel, top),
        out_shape=wire_shape,
        in_specs=[smem(), smem(), vmem()],
        out_specs=vmem(),
        name="weigh",
    )(position, gates, cot_tiles)
    routed_recv = exchange(routed_send)

    replicas = lax.axis_size("dp")
    here = lax.axis_index("dp")

    def to_replica(x, step):
        return lax.ppermute(x, "dp", [(i, (i + step) % replicas) for i in range(replicas)])

    def gather_replicas(shard, axis):
        size = shard.shape[axis]
        shape = list(shard.shape)
        shape[axis] = size * replicas
        full = jnp.zeros(shape, shard.dtype)
        for step in range(replicas):
            piece = to_replica(shard, step) if step else shard
            place = (here - step) % replicas * size
            full = lax.dynamic_update_slice_in_dim(full, piece, place, axis)
        return full

    def sum_replicas(part, axis):
        size = part.shape[axis] // replicas
        total = None
        for step in range(replicas):
            place = (here + step) % replicas * size
            piece = lax.dynamic_slice_in_dim(part, place, size, axis)
            piece = to_replica(piece, step) if step else piece
            piece = piece.astype(f32)
            total = piece if total is None else total + piece
        return total

    hid = w_gate.shape[2]
    full_in = gather_replicas(jnp.concatenate([w_gate[0], w_up[0]], axis=1), 0)
    full_down = gather_replicas(w_down[0], 1)

    def dot(a, b, dims):
        return lax.dot_general(a, b, (dims, ((), ())), preferred_element_type=f32)

    rows_in = to_rows(token_recv, width)
    pre = dot(rows_in, full_in, ((1,), (0,)))
    pre_gate, pre_up = pre[:, :hid], pre[:, hid:]
    activated, _ = silu_parts(pre_gate)
    hidden = (activated * pre_up).astype(bf16)
    expert_out = dot(hidden, full_down, ((1,), (0,))).astype(bf16)
    out_send = to_wire(expert_out, sub)
    back_out = exchange(out_send)

    routed_recv, pre, _ = lax.optimization_barrier((routed_recv, pre, out_send))
    pre_gate, pre_up = pre[:, :hid], pre[:, hid:]
    activated, slope = silu_parts(pre_gate)
    routed_in = to_rows(routed_recv, width)
    grad_hidden = dot(routed_in, full_down, ((1,), (1,)))
    grad_pre = jnp.concatenate(
        [
            (grad_hidden * pre_up * slope).astype(bf16),
            (grad_hidden * activated).astype(bf16),
        ],
        axis=1,
    )
    pair_grad = dot(grad_pre, full_in, ((1,), (1,))).astype(bf16)
    grad_send = to_wire(pair_grad, sub)
    back_grad = exchange(grad_send)

    def weight_part(a, b):
        return dot(a, b, ((0,), (0,))).astype(bf16)

    grad_down_w = sum_replicas(weight_part(hidden, routed_in), 1)[None]
    grad_in = sum_replicas(weight_part(rows_in, grad_pre), 0)
    grad_gate_w, grad_up_w = grad_in[None, :, :hid], grad_in[None, :, hid:]

    mixed, dots = call(
        functools.partial(mix_kernel, top),
        out_shape=(token_shape, jax.ShapeDtypeStruct((rows * top, LANES), f32)),
        in_specs=[smem(), smem(), vmem(), vmem()],
        out_specs=(vmem(), vmem()),
        name="mix",
    )(position, gates, cot_tiles, back_out)
    grad_gates = jnp.sum(dots, axis=1).reshape(top, rows).T

    mixed, back_grad = lax.optimization_barrier((to_rows(mixed, width), back_grad))
    grad_tokens = call(
        functools.partial(gather_sum_kernel, top),
        out_shape=token_shape,
        in_specs=[smem(), vmem()],
        out_specs=vmem(),
        name="gather_sum",
    )(position, back_grad)
    return (
        mixed,
        to_rows(grad_tokens, width),
        grad_gates,
        grad_gate_w,
        grad_up_w,
        grad_down_w,
    )


def solution(mesh):
    tokens = P(("dp", "expert"), None)
    first = P("expert", "dp", None)
    last = P("expert", None, "dp")

    return jax.shard_map(
        on_device,
        mesh=mesh,
        in_specs=(tokens, tokens, tokens, tokens, first, first, last),
        out_specs=(tokens, tokens, tokens, first, first, last),
        check_vma=False,
    )
```

```python
import functools

import jax
import jax.numpy as jnp
from jax import lax
from jax.experimental import pallas as pl
from jax.experimental.pallas import tpu as pltpu
from jax.sharding import PartitionSpec as P


INTERPRET = False
LANES = 128


def smem():
    return pl.BlockSpec(memory_space=pltpu.SMEM)


def vmem():
    return pl.BlockSpec(memory_space=pltpu.VMEM)


def clear_rows(out_ref, step=80):
    rows = out_ref.shape[0]
    zero = jnp.zeros((step,) + out_ref.shape[1:], out_ref.dtype)

    def body(i, carry):
        out_ref[pl.ds(i * step, step)] = zero
        return carry

    lax.fori_loop(0, rows // step, body, 0)


def for_each(count, body, unroll=4):
    def step(i, carry):
        for j in range(unroll):
            body(unroll * i + j)
        return carry

    lax.fori_loop(0, count // unroll, step, 0)


def route_kernel(capacity, experts, ids_ref, tok_ref, out_ref, pos_ref, place_ref, tile_ref, sem):
    top, rows = ids_ref.shape
    f32 = jnp.float32
    expert = lax.broadcasted_iota(jnp.int32, (experts, rows), 0)
    hits = [ids_ref[pl.ds(k, 1), :] == expert for k in range(top)]
    named = sum(hit.astype(f32) for hit in hits).astype(jnp.bfloat16)
    first = lax.broadcasted_iota(jnp.int32, (rows, rows), 0)
    second = lax.broadcasted_iota(jnp.int32, (rows, rows), 1)
    before = (first < second).astype(f32).astype(jnp.bfloat16)
    rank = jnp.dot(named, before, preferred_element_type=f32)
    slot = (expert * capacity).astype(f32) + rank
    for k in range(top):
        chosen = jnp.sum(jnp.where(hits[k], slot, 0.0), axis=0, keepdims=True)
        pos_ref[pl.ds(k, 1), :] = chosen.astype(jnp.int32)
    copy = pltpu.make_async_copy(pos_ref, place_ref, sem)
    copy.start()
    tile_ref[...] = tok_ref[...].reshape(tile_ref.shape)
    clear_rows(out_ref)
    copy.wait()

    def body(t):
        row = tile_ref[t]
        for k in range(top):
            out_ref[place_ref[k, t]] = row

    for_each(rows, body, 16)


def weigh_kernel(top, pos_ref, gate_ref, cot_ref, out_ref):
    clear_rows(out_ref)

    def body(t, carry):
        row = cot_ref[t].astype(jnp.float32)
        for k in range(top):
            out_ref[pos_ref[k, t]] = (row * gate_ref[k, t]).astype(jnp.bfloat16)
        return carry

    lax.fori_loop(0, cot_ref.shape[0], body, 0)


def mix_kernel(top, pos_ref, gate_ref, cot_ref, back_ref, mixed_ref, dots_ref):
    rows = cot_ref.shape[0]

    def body(t, carry):
        cot = cot_ref[t].astype(jnp.float32)
        total = jnp.zeros(cot.shape, jnp.float32)
        for k in range(top):
            row = back_ref[pos_ref[k, t]].astype(jnp.float32)
            total = total + row * gate_ref[k, t]
            dots_ref[pl.ds(k * rows + t, 1), :] = jnp.sum(row * cot, axis=0, keepdims=True)
        mixed_ref[t] = total.astype(jnp.bfloat16)
        return carry

    lax.fori_loop(0, cot_ref.shape[0], body, 0)


def gather_sum_kernel(top, pos_ref, back_ref, out_ref, tile_ref):
    def body(t):
        total = back_ref[pos_ref[0, t]].astype(jnp.float32)
        for k in range(1, top):
            total = total + back_ref[pos_ref[k, t]].astype(jnp.float32)
        tile_ref[t] = total.astype(jnp.bfloat16)

    for_each(out_ref.shape[0], body, 16)
    out_ref[...] = tile_ref[...].reshape(out_ref.shape)


def silu_parts(pre_gate):
    sigma = jax.nn.sigmoid(pre_gate)
    return (pre_gate * sigma, sigma * (1.0 + pre_gate * (1.0 - sigma)))


def to_rows(wire, width):
    return wire.reshape(-1, width)


def to_wire(rows, sublanes):
    return rows.reshape(-1, sublanes, LANES)


def on_device(tokens, cotangent, expert_ids, gate_probs, w_gate, w_up, w_down):
    group = lax.axis_size("expert")
    all_experts = w_gate.shape[0] * group
    rows, width = tokens.shape
    top = expert_ids.shape[1]
    capacity = max(2, 5 * rows * top // (4 * all_experts))
    slots = all_experts * capacity
    sub = width // LANES
    f32, bf16 = jnp.float32, jnp.bfloat16

    def exchange(x):
        chunks = x.reshape(group, capacity * sub, LANES)
        return lax.all_to_all(chunks, "expert", 0, 0, tiled=True).reshape(slots, sub, LANES)

    wire_shape = jax.ShapeDtypeStruct((slots, sub, LANES), bf16)
    token_shape = jax.ShapeDtypeStruct((rows, sub, LANES), bf16)
    params = pltpu.CompilerParams(vmem_limit_bytes=32 << 20)
    call = functools.partial(pl.pallas_call, compiler_params=params, interpret=INTERPRET)

    gates = gate_probs.T.astype(f32)
    cot_tiles = to_wire(cotangent, sub)

    token_send, position = call(
        functools.partial(route_kernel, capacity, all_experts),
        out_shape=(wire_shape, jax.ShapeDtypeStruct((top, rows), jnp.int32)),
        in_specs=[vmem(), vmem()],
        out_specs=(vmem(), vmem()),
        scratch_shapes=[pltpu.SMEM((top, rows), jnp.int32), pltpu.VMEM((rows, sub, LANES), bf16), pltpu.SemaphoreType.DMA],
        name="route",
    )(expert_ids.T, tokens)
    token_recv = exchange(token_send)

    routed_send = call(
        functools.partial(weigh_kernel, top),
        out_shape=wire_shape,
        in_specs=[smem(), smem(), vmem()],
        out_specs=vmem(),
        name="weigh",
    )(position, gates, cot_tiles)
    routed_recv = exchange(routed_send)

    replicas = lax.axis_size("dp")
    here = lax.axis_index("dp")

    def to_replica(x, step):
        return lax.ppermute(x, "dp", [(i, (i + step) % replicas) for i in range(replicas)])

    def gather_replicas(shard, axis):
        size = shard.shape[axis]
        shape = list(shard.shape)
        shape[axis] = size * replicas
        full = jnp.zeros(shape, shard.dtype)
        for step in range(replicas):
            piece = to_replica(shard, step) if step else shard
            place = (here - step) % replicas * size
            full = lax.dynamic_update_slice_in_dim(full, piece, place, axis)
        return full

    def sum_replicas(part, axis):
        size = part.shape[axis] // replicas
        total = None
        for step in range(replicas):
            place = (here + step) % replicas * size
            piece = lax.dynamic_slice_in_dim(part, place, size, axis)
            piece = to_replica(piece, step) if step else piece
            piece = piece.astype(f32)
            total = piece if total is None else total + piece
        return total

    hid = w_gate.shape[2]
    full_in = gather_replicas(jnp.concatenate([w_gate[0], w_up[0]], axis=1), 0)
    full_down = gather_replicas(w_down[0], 1)

    def dot(a, b, dims):
        return lax.dot_general(a, b, (dims, ((), ())), preferred_element_type=f32)

    rows_in = to_rows(token_recv, width)
    pre = dot(rows_in, full_in, ((1,), (0,)))
    pre_gate, pre_up = pre[:, :hid], pre[:, hid:]
    activated, _ = silu_parts(pre_gate)
    hidden = (activated * pre_up).astype(bf16)
    expert_out = dot(hidden, full_down, ((1,), (0,))).astype(bf16)
    out_send = to_wire(expert_out, sub)
    back_out = exchange(out_send)

    routed_recv, pre, _ = lax.optimization_barrier((routed_recv, pre, out_send))
    pre_gate, pre_up = pre[:, :hid], pre[:, hid:]
    activated, slope = silu_parts(pre_gate)
    routed_in = to_rows(routed_recv, width)
    grad_hidden = dot(routed_in, full_down, ((1,), (1,)))
    grad_pre = jnp.concatenate(
        [
            (grad_hidden * pre_up * slope).astype(bf16),
            (grad_hidden * activated).astype(bf16),
        ],
        axis=1,
    )
    pair_grad = dot(grad_pre, full_in, ((1,), (1,))).astype(bf16)
    grad_send = to_wire(pair_grad, sub)
    back_grad = exchange(grad_send)

    def weight_part(a, b):
        return dot(a, b, ((0,), (0,))).astype(bf16)

    grad_down_w = sum_replicas(weight_part(hidden, routed_in), 1)[None]
    grad_in = sum_replicas(weight_part(rows_in, grad_pre), 0)
    grad_gate_w, grad_up_w = grad_in[None, :, :hid], grad_in[None, :, hid:]

    mixed, dots = call(
        functools.partial(mix_kernel, top),
        out_shape=(token_shape, jax.ShapeDtypeStruct((rows * top, LANES), f32)),
        in_specs=[smem(), smem(), vmem(), vmem()],
        out_specs=(vmem(), vmem()),
        name="mix",
    )(position, gates, cot_tiles, back_out)
    grad_gates = jnp.sum(dots, axis=1).reshape(top, rows).T

    mixed, back_grad = lax.optimization_barrier((to_rows(mixed, width), back_grad))
    grad_tokens = call(
        functools.partial(gather_sum_kernel, top),
        out_shape=jax.ShapeDtypeStruct((rows, width), bf16),
        in_specs=[smem(), vmem()],
        out_specs=vmem(),
        scratch_shapes=[pltpu.VMEM((rows, sub, LANES), bf16)],
        name="gather_sum",
    )(position, back_grad)
    return (
        mixed,
        grad_tokens,
        grad_gates,
        grad_gate_w,
        grad_up_w,
        grad_down_w,
    )


def solution(mesh):
    tokens = P(("dp", "expert"), None)
    first = P("expert", "dp", None)
    last = P("expert", None, "dp")

    return jax.shard_map(
        on_device,
        mesh=mesh,
        in_specs=(tokens, tokens, tokens, tokens, first, first, last),
        out_specs=(tokens, tokens, tokens, first, first, last),
        check_vma=False,
    )
```

```python
import functools

import jax
import jax.numpy as jnp
from jax import lax
from jax.experimental import pallas as pl
from jax.experimental.pallas import tpu as pltpu
from jax.sharding import PartitionSpec as P


INTERPRET = False
LANES = 128


def smem():
    return pl.BlockSpec(memory_space=pltpu.SMEM)


def vmem():
    return pl.BlockSpec(memory_space=pltpu.VMEM)


def clear_rows(out_ref, step=80):
    rows = out_ref.shape[0]
    zero = jnp.zeros((step,) + out_ref.shape[1:], out_ref.dtype)

    def body(i, carry):
        out_ref[pl.ds(i * step, step)] = zero
        return carry

    lax.fori_loop(0, rows // step, body, 0)


def for_each(count, body, unroll=4):
    def step(i, carry):
        for j in range(unroll):
            body(unroll * i + j)
        return carry

    lax.fori_loop(0, count // unroll, step, 0)


def route_kernel(capacity, experts, ids_ref, tok_ref, out_ref, pos_ref, place_ref, tile_ref, sem):
    top, rows = ids_ref.shape
    f32 = jnp.float32
    expert = lax.broadcasted_iota(jnp.int32, (experts, rows), 0)
    hits = [ids_ref[pl.ds(k, 1), :] == expert for k in range(top)]
    named = sum(hit.astype(f32) for hit in hits).astype(jnp.bfloat16)
    first = lax.broadcasted_iota(jnp.int32, (rows, rows), 0)
    second = lax.broadcasted_iota(jnp.int32, (rows, rows), 1)
    before = (first < second).astype(f32).astype(jnp.bfloat16)
    rank = jnp.dot(named, before, preferred_element_type=f32)
    slot = (expert * capacity).astype(f32) + rank
    for k in range(top):
        chosen = jnp.sum(jnp.where(hits[k], slot, 0.0), axis=0, keepdims=True)
        pos_ref[pl.ds(k, 1), :] = chosen.astype(jnp.int32)
    copy = pltpu.make_async_copy(pos_ref, place_ref, sem)
    copy.start()
    tile_ref[...] = tok_ref[...].reshape(tile_ref.shape)
    clear_rows(out_ref)
    copy.wait()

    def body(t):
        row = tile_ref[t]
        for k in range(top):
            out_ref[place_ref[k, t]] = row

    for_each(rows, body, 16)


def weigh_kernel(top, pos_ref, gate_ref, cot_ref, out_ref):
    clear_rows(out_ref)

    def body(t, carry):
        row = cot_ref[t].astype(jnp.float32)
        for k in range(top):
            out_ref[pos_ref[k, t]] = (row * gate_ref[k, t]).astype(jnp.bfloat16)
        return carry

    lax.fori_loop(0, cot_ref.shape[0], body, 0)


def mix_kernel(top, pos_ref, gate_ref, cot_ref, back_ref, mixed_ref, dots_ref):
    rows = cot_ref.shape[0]

    def body(t, carry):
        cot = cot_ref[t].astype(jnp.float32)
        total = jnp.zeros(cot.shape, jnp.float32)
        for k in range(top):
            row = back_ref[pos_ref[k, t]].astype(jnp.float32)
            total = total + row * gate_ref[k, t]
            dots_ref[pl.ds(k * rows + t, 1), :] = jnp.sum(row * cot, axis=0, keepdims=True)
        mixed_ref[t] = total.astype(jnp.bfloat16)
        return carry

    lax.fori_loop(0, cot_ref.shape[0], body, 0)


def gather_sum_kernel(top, pos_ref, back_ref, out_ref, tile_ref):
    base = pl.program_id(0) * out_ref.shape[0]

    def body(t):
        total = back_ref[pos_ref[0, base + t]].astype(jnp.float32)
        for k in range(1, top):
            total = total + back_ref[pos_ref[k, base + t]].astype(jnp.float32)
        tile_ref[t] = total.astype(jnp.bfloat16)

    for_each(out_ref.shape[0], body, 16)
    out_ref[...] = tile_ref[...].reshape(out_ref.shape)


def silu_parts(pre_gate):
    sigma = jax.nn.sigmoid(pre_gate)
    return (pre_gate * sigma, sigma * (1.0 + pre_gate * (1.0 - sigma)))


def to_rows(wire, width):
    return wire.reshape(-1, width)


def to_wire(rows, sublanes):
    return rows.reshape(-1, sublanes, LANES)


def on_device(tokens, cotangent, expert_ids, gate_probs, w_gate, w_up, w_down):
    group = lax.axis_size("expert")
    all_experts = w_gate.shape[0] * group
    rows, width = tokens.shape
    top = expert_ids.shape[1]
    capacity = max(2, 5 * rows * top // (4 * all_experts))
    slots = all_experts * capacity
    sub = width // LANES
    f32, bf16 = jnp.float32, jnp.bfloat16

    def exchange(x):
        chunks = x.reshape(group, capacity * sub, LANES)
        return lax.all_to_all(chunks, "expert", 0, 0, tiled=True).reshape(slots, sub, LANES)

    wire_shape = jax.ShapeDtypeStruct((slots, sub, LANES), bf16)
    token_shape = jax.ShapeDtypeStruct((rows, sub, LANES), bf16)
    params = pltpu.CompilerParams(vmem_limit_bytes=32 << 20)
    call = functools.partial(pl.pallas_call, compiler_params=params, interpret=INTERPRET)

    gates = gate_probs.T.astype(f32)
    cot_tiles = to_wire(cotangent, sub)

    token_send, position = call(
        functools.partial(route_kernel, capacity, all_experts),
        out_shape=(wire_shape, jax.ShapeDtypeStruct((top, rows), jnp.int32)),
        in_specs=[vmem(), vmem()],
        out_specs=(vmem(), vmem()),
        scratch_shapes=[pltpu.SMEM((top, rows), jnp.int32), pltpu.VMEM((rows, sub, LANES), bf16), pltpu.SemaphoreType.DMA],
        name="route",
    )(expert_ids.T, tokens)
    token_recv = exchange(token_send)

    routed_send = call(
        functools.partial(weigh_kernel, top),
        out_shape=wire_shape,
        in_specs=[smem(), smem(), vmem()],
        out_specs=vmem(),
        name="weigh",
    )(position, gates, cot_tiles)
    routed_recv = exchange(routed_send)

    replicas = lax.axis_size("dp")
    here = lax.axis_index("dp")

    def to_replica(x, step):
        return lax.ppermute(x, "dp", [(i, (i + step) % replicas) for i in range(replicas)])

    def gather_replicas(shard, axis):
        size = shard.shape[axis]
        shape = list(shard.shape)
        shape[axis] = size * replicas
        full = jnp.zeros(shape, shard.dtype)
        for step in range(replicas):
            piece = to_replica(shard, step) if step else shard
            place = (here - step) % replicas * size
            full = lax.dynamic_update_slice_in_dim(full, piece, place, axis)
        return full

    def sum_replicas(part, axis):
        size = part.shape[axis] // replicas
        total = None
        for step in range(replicas):
            place = (here + step) % replicas * size
            piece = lax.dynamic_slice_in_dim(part, place, size, axis)
            piece = to_replica(piece, step) if step else piece
            piece = piece.astype(f32)
            total = piece if total is None else total + piece
        return total

    hid = w_gate.shape[2]
    full_in = gather_replicas(jnp.concatenate([w_gate[0], w_up[0]], axis=1), 0)
    full_down = gather_replicas(w_down[0], 1)

    def dot(a, b, dims):
        return lax.dot_general(a, b, (dims, ((), ())), preferred_element_type=f32)

    rows_in = to_rows(token_recv, width)
    pre = dot(rows_in, full_in, ((1,), (0,)))
    pre_gate, pre_up = pre[:, :hid], pre[:, hid:]
    activated, _ = silu_parts(pre_gate)
    hidden = (activated * pre_up).astype(bf16)
    expert_out = dot(hidden, full_down, ((1,), (0,))).astype(bf16)
    out_send = to_wire(expert_out, sub)
    back_out = exchange(out_send)

    routed_recv, pre, _ = lax.optimization_barrier((routed_recv, pre, out_send))
    pre_gate, pre_up = pre[:, :hid], pre[:, hid:]
    activated, slope = silu_parts(pre_gate)
    routed_in = to_rows(routed_recv, width)
    grad_hidden = dot(routed_in, full_down, ((1,), (1,)))
    grad_pre = jnp.concatenate(
        [
            (grad_hidden * pre_up * slope).astype(bf16),
            (grad_hidden * activated).astype(bf16),
        ],
        axis=1,
    )
    pair_grad = dot(grad_pre, full_in, ((1,), (1,))).astype(bf16)
    grad_send = to_wire(pair_grad, sub)
    back_grad = exchange(grad_send)

    def weight_part(a, b):
        return dot(a, b, ((0,), (0,))).astype(bf16)

    grad_down_w = sum_replicas(weight_part(hidden, routed_in), 1)[None]
    grad_in = sum_replicas(weight_part(rows_in, grad_pre), 0)
    grad_gate_w, grad_up_w = grad_in[None, :, :hid], grad_in[None, :, hid:]

    mixed, dots = call(
        functools.partial(mix_kernel, top),
        out_shape=(token_shape, jax.ShapeDtypeStruct((rows * top, LANES), f32)),
        in_specs=[smem(), smem(), vmem(), vmem()],
        out_specs=(vmem(), vmem()),
        name="mix",
    )(position, gates, cot_tiles, back_out)
    grad_gates = jnp.sum(dots, axis=1).reshape(top, rows).T

    mixed, back_grad = lax.optimization_barrier((to_rows(mixed, width), back_grad))
    part = rows // 4 if rows % 64 == 0 else rows
    grad_tokens = call(
        functools.partial(gather_sum_kernel, top),
        out_shape=jax.ShapeDtypeStruct((rows, width), bf16),
        grid=(rows // part,),
        in_specs=[smem(), vmem()],
        out_specs=pl.BlockSpec((part, width), lambda i: (i, 0)),
        scratch_shapes=[pltpu.VMEM((part, sub, LANES), bf16)],
        name="gather_sum",
    )(position, back_grad)
    return (
        mixed,
        grad_tokens,
        grad_gates,
        grad_gate_w,
        grad_up_w,
        grad_down_w,
    )


def solution(mesh):
    tokens = P(("dp", "expert"), None)
    first = P("expert", "dp", None)
    last = P("expert", None, "dp")

    return jax.shard_map(
        on_device,
        mesh=mesh,
        in_specs=(tokens, tokens, tokens, tokens, first, first, last),
        out_specs=(tokens, tokens, tokens, first, first, last),
        check_vma=False,
    )
```
